256 devices in a mesh: shard: 64 (over y, z_lo, x, core), tensor: 4 (over z_hi).
Axes of the slice: x: 4, y: 4, z: 8 (z_hi: 4, z_lo: 2; z = z_hi * 2 + z_lo), core: 2. Of those that a mesh axis runs over, the one named last changes fastest.
Arguments:
- grads: bfloat16 [256, 1024, 1024], P(None, 'shard', 'tensor'), may hold values from -48 to 48
- momentum: float32 [256, 1024, 1024], P(None, 'shard', 'tensor'), may hold values from -6 to 6
Outputs:
- momentum_next: float32 [256, 1024, 1024], P(None, 'shard', 'tensor')
- update: bfloat16 [256, 1024, 1024], P(None, 'shard', 'tensor')
The draws below stay inside these ranges and needn't reach their ends.
All inputs are finite; a program needn't handle non-finite values.
Results may differ from the reference program's by a relative error of at most 0.012.
Values may be sent and summed in bfloat16 or wider, within the bound.
A program may use at most 64 MiB of HBM per device.

```python
import jax
import jax.numpy as jnp
from jax import lax

D = 1024
NS_STEPS = 2
MATS = 256


def draw_grads(key, part):
    key_base, key_rows, key_cols = jax.random.split(jax.random.fold_in(key, 17), 3)
    rows = jnp.exp(jax.random.uniform(key_rows, (MATS, D, 1), jnp.float32) * 2.302585) / 3.1622777
    cols = jnp.exp(jax.random.uniform(key_cols, (MATS, 1, D), jnp.float32) * 2.302585) / 3.1622777
    base = jnp.clip(jax.random.normal(key_base, (MATS, D, D), jnp.float32), -4.0, 4.0)
    return (base * rows * cols).astype(jnp.bfloat16)


def steps_of(own_key, extent, cuts, smallest, top_value):
    factor_of, own = 1.0, jax.random.fold_in(own_key, 6)
    for dim, blocks in cuts:
        draws = jnp.exp(jax.random.uniform(jax.random.fold_in(own, dim), (blocks,), jnp.float32, smallest / len(cuts), top_value / len(cuts)))
        factor_of = factor_of * jnp.repeat(draws, extent[dim] // blocks).reshape([-1 if axis == dim else 1 for axis in range(len(extent))])
    return factor_of


def bell_draw(own_key, shape, deviation, most, cuts=(), dtype=jnp.bfloat16):
    entries = jax.random.normal(own_key, shape, jnp.float32) * deviation
    if len(cuts) > 0:
        entries = steps_of(own_key, shape, cuts, -0.22, 0.18) * entries
    return jnp.clip(entries, min=-most, max=most).astype(dtype)


def setup_inputs(seed: int = 0) -> dict:
    splits = jax.random.split(jax.random.key(seed), 3)
    return {
        "grads": draw_grads(jax.random.fold_in(splits[2], 71), 0),
        "momentum": bell_draw(splits[1], (MATS, D, D), 1.0, 6.0, ((1, 64), (2, 4)), jnp.float32),
    }


def dot32(left, right):
    return jnp.dot(left.astype(jnp.float32), right.astype(jnp.float32), precision=lax.Precision.HIGHEST)

def orthogonalize(nesterov):
    values = nesterov.astype(jnp.float32)
    norm_value = jnp.sqrt(jnp.sum(values * values))
    current = (values / (norm_value + 1e-07)).astype(jnp.bfloat16)
    for step in range(NS_STEPS):
        gram = dot32(current, current.T).astype(jnp.bfloat16)
        power_f = dot32(gram, current)
        power = power_f.astype(jnp.bfloat16)
        square = dot32(gram, power)
        current = (3.4445 * current.astype(jnp.float32) - 4.775 * power_f + 2.0315 * square).astype(jnp.bfloat16)
    scale = 0.2 * float(D) ** 0.5
    return (scale * current.astype(jnp.float32)).astype(jnp.bfloat16)

def reference(grads, momentum):
    momentum_next = 0.95 * momentum + grads.astype(jnp.float32)
    nesterov = (grads.astype(jnp.float32) + 0.95 * momentum_next).astype(jnp.bfloat16)
    update = lax.map(orthogonalize, nesterov)
    return (momentum_next, update)
```

```python
import functools

import jax
import jax.numpy as jnp
from jax import lax
from jax.experimental import pallas as pl
from jax.experimental.pallas import tpu as pltpu
from jax.sharding import PartitionSpec as P

MESH = pl.DeviceIdType.MESH
NT = (((1,), (1,)), ((), ()))
A, B, C = 3.4445, -4.775, 2.0315
HOPS = (4, 1, -1, 2, -2, 3, -3, 0)


def place():
    shard = lax.axis_index("shard")
    tensor = lax.axis_index("tensor")
    return (shard // 2) % 4, shard // 16, tensor * 2 + (shard // 8) % 2, shard % 2


def mesh_index(x, y, z, core):
    return y * 16 + (z % 2) * 8 + x * 2 + core, z // 2


def dot(left, right, dims=(((1,), (0,)), ((), ()))):
    return lax.dot_general(left, right, dims, preferred_element_type=jnp.float32)


def kernel(nest, out, whole, gram_f, gram, poly, mid, upd, send_sem, recv_sem, back_send_sem, back_recv_sem):
    my_shard, my_tensor = lax.axis_index("shard"), lax.axis_index("tensor")
    me = my_shard * 4 + my_tensor
    x, y, z, core = place()

    barrier = pltpu.get_barrier_semaphore()

    def greet(step, carry):
        to = (lax.rem(my_shard + step // 4, 64), lax.rem(my_tensor + step % 4, 4))
        pl.semaphore_signal(barrier, inc=1, device_id=to, device_id_type=MESH)
        return carry

    lax.fori_loop(1, 256, greet, 0)
    pl.semaphore_wait(barrier, 255)

    own = pltpu.make_async_copy(nest.at[me], whole.at[my_tensor, my_shard], recv_sem)
    own.start()

    def forward(to_x, to_y, to_z, to_core):
        shard, tensor = mesh_index(to_x, to_y, to_z, to_core)
        pltpu.make_async_remote_copy(
            src_ref=nest.at[shard * 4 + tensor],
            dst_ref=whole.at[my_tensor, my_shard],
            send_sem=send_sem,
            recv_sem=recv_sem,
            device_id=(shard, tensor),
            device_id_type=MESH,
        ).start()

    for to_core in (0, 1):

        def to_plane(step, carry, to_core=to_core):
            to_x, to_y = (x + step) % 4, (y + step // 4) % 4
            for hop in HOPS:
                if hop == 0:

                    @pl.when((step > 0) | (core != to_core))
                    def _():
                        forward(to_x, to_y, z, to_core)
                else:
                    forward(to_x, to_y, (z + hop) % 8, to_core)
            return carry

        lax.fori_loop(0, 16, to_plane, 0)

    pltpu.make_async_copy(whole, whole, recv_sem).wait()

    def panel(ref, t, i):
        return ref[t, pl.ds(i * 16, 16)].reshape(256, 256)

    def make_gram(ref, i):
        total = None
        for t in range(4):
            part = dot(panel(ref, t, i), ref[t].reshape(1024, 256), NT)
            total = part if total is None else total + part
        return total

    def rows(i):
        return pl.ds(pl.multiple_of(i * 256, 256), 256)

    def first_gram(i, carry):
        gram_f[rows(i), :] = make_gram(whole, i)
        return carry

    lax.fori_loop(0, 4, first_gram, 0)
    squares = jnp.zeros((256, 256), jnp.float32)
    diagonal = lax.broadcasted_iota(jnp.int32, (256, 256), 0) == lax.broadcasted_iota(jnp.int32, (256, 256), 1)
    for i in range(4):
        squares += jnp.where(diagonal, gram_f[256 * i : 256 * i + 256, 256 * i : 256 * i + 256], 0.0)
    norm = jnp.sqrt(jnp.sum(squares, keepdims=True))
    scale = 1.0 / (norm + 1e-7)

    def round_gram(i, carry):
        gram[rows(i), :] = (gram_f[rows(i), :] * (scale * scale)).astype(jnp.bfloat16)
        return carry

    lax.fori_loop(0, 4, round_gram, 0)

    def make_poly(i, carry):
        strip = gram[rows(i), :]
        poly[rows(i), :] = (B * strip.astype(jnp.float32) + C * dot(strip, gram[...])).astype(jnp.bfloat16)
        return carry

    lax.fori_loop(0, 4, make_poly, 0)

    def first_step(i, carry):
        for t in range(4):
            value = A * panel(whole, t, i).astype(jnp.float32) + dot(poly[rows(i), :], whole[t].reshape(1024, 256))
            mid[t, pl.ds(i * 16, 16)] = (value * scale).astype(jnp.bfloat16).reshape(16, 16, 256)
        return carry

    lax.fori_loop(0, 4, first_step, 0)

    def second_gram(i, carry):
        gram[rows(i), :] = make_gram(mid, i).astype(jnp.bfloat16)
        return carry

    lax.fori_loop(0, 4, second_gram, 0)
    lax.fori_loop(0, 4, make_poly, 0)

    def backward(to_x, to_y, to_z, to_core):
        shard, tensor = mesh_index(to_x, to_y, to_z, to_core)
        pltpu.make_async_remote_copy(
            src_ref=upd.at[tensor, shard],
            dst_ref=out.at[me],
            send_sem=back_send_sem,
            recv_sem=back_recv_sem,
            device_id=(shard, tensor),
            device_id_type=MESH,
        ).start()

    def second_step(step, carry):
        to_y = (y + step) % 4
        for t in range(4):
            value = A * panel(mid, t, to_y).astype(jnp.float32) + dot(poly[rows(to_y), :], mid[t].reshape(1024, 256))
            upd[t, pl.ds(to_y * 16, 16)] = (0.2 * 32.0 * value).astype(jnp.bfloat16).reshape(16, 16, 256)

        def to_line(line, carry):
            to_x, to_core = (x + line // 2) % 4, (core + line) % 2
            for hop in HOPS:
                if hop == 0:

                    @pl.when((step > 0) | (line > 0))
                    def _():
                        backward(to_x, to_y, z, to_core)
                else:
                    backward(to_x, to_y, (z + hop) % 8, to_core)
            return carry

        lax.fori_loop(0, 8, to_line, 0)
        return carry

    lax.fori_loop(0, 4, second_step, 0)
    kept = pltpu.make_async_copy(upd.at[my_tensor, my_shard], out.at[me], back_recv_sem)
    kept.start()

    sent = nest.at[pl.ds(0, 255)]
    pltpu.make_async_copy(sent, sent, send_sem).wait()
    pltpu.make_async_copy(sent, sent, back_send_sem).wait()
    pltpu.make_async_copy(out, out, back_recv_sem).wait()


def shards(grads, momentum):
    grads_f = grads.astype(jnp.float32)
    momentum_next = 0.95 * momentum + grads_f
    nesterov = (grads_f + 0.95 * momentum_next).astype(jnp.bfloat16)
    vmem = pl.BlockSpec(memory_space=pltpu.VMEM)
    panels = (4, 64, 16, 256)
    update = pl.pallas_call(
        kernel,
        name="muon",
        out_shape=jax.ShapeDtypeStruct(nesterov.shape, jnp.bfloat16),
        in_specs=[vmem],
        out_specs=vmem,
        scratch_shapes=[
            pltpu.VMEM(panels, jnp.bfloat16),
            pltpu.VMEM((1024, 1024), jnp.float32),
            pltpu.VMEM((1024, 1024), jnp.bfloat16),
            pltpu.VMEM((1024, 1024), jnp.bfloat16),
            pltpu.VMEM(panels, jnp.bfloat16),
            pltpu.VMEM(panels, jnp.bfloat16),
            pltpu.SemaphoreType.DMA,
            pltpu.SemaphoreType.DMA,
            pltpu.SemaphoreType.DMA,
            pltpu.SemaphoreType.DMA,
        ],
        compiler_params=pltpu.CompilerParams(collective_id=0, has_side_effects=True),
    )(nesterov)
    return (momentum_next, update)


def solution(mesh):
    spec = P(None, "shard", "tensor")
    return jax.shard_map(shards, mesh=mesh, in_specs=(spec, spec), out_specs=(spec, spec), check_vma=False)
```

```python
import jax
import jax.numpy as jnp
from jax import lax
from jax.experimental import pallas as pl
from jax.experimental.pallas import tpu as pltpu
from jax.sharding import PartitionSpec as P

MESH = pl.DeviceIdType.MESH
NT = (((1,), (1,)), ((), ()))
A, B, C = 3.4445, -4.775, 2.0315
CHUNK = 32
HOPS = (4, 1, -1, 2, -2, 3, -3, 0)


def place():
    shard = lax.axis_index("shard")
    tensor = lax.axis_index("tensor")
    return (shard // 2) % 4, shard // 16, tensor * 2 + (shard // 8) % 2, shard % 2


def mesh_index(x, y, z, core):
    return y * 16 + (z % 2) * 8 + x * 2 + core, z // 2


def dot(left, right, dims=(((1,), (0,)), ((), ()))):
    return lax.dot_general(left, right, dims, preferred_element_type=jnp.float32)


def kernel(grads, momentum, kept, out, fresh, nest, whole, gram_f, gram, poly, mid, upd, load_sem, send_sem, recv_sem, back_send_sem, back_recv_sem):
    my_shard, my_tensor = lax.axis_index("shard"), lax.axis_index("tensor")
    me = my_shard * 4 + my_tensor
    x, y, z, core = place()

    def load(i):
        part = pl.ds(i * CHUNK, CHUNK)
        return (
            pltpu.make_async_copy(grads.at[part], fresh.at[part], load_sem.at[0, i]),
            pltpu.make_async_copy(momentum.at[part], kept.at[part], load_sem.at[1, i]),
        )

    for i in range(256 // CHUNK):
        for copy in load(i):
            copy.start()

    barrier = pltpu.get_barrier_semaphore()
    depths = [(z + hop) % 8 for hop in (4, 3, 5, 2, 6, 1, 7, 0)]
    depths = [((depth % 2) * 8, depth // 2) for depth in depths]

    def greet(step, carry):
        column = ((y + 2 + step // 4) % 4) * 16 + ((x + 2 + step) % 4) * 2
        for low, tensor in depths:
            for other in (0, 1):
                shard = column + low + other

                @pl.when((shard != my_shard) | (tensor != my_tensor))
                def _():
                    pl.semaphore_signal(barrier, inc=1, device_id=(shard, tensor), device_id_type=MESH)
        return carry

    lax.fori_loop(0, 16, greet, 0)

    def blend(i, carry):
        for copy in load(i):
            copy.wait()
        part = pl.ds(i * CHUNK, CHUNK)
        grads_f = fresh[part].astype(jnp.float32)
        momentum_next = 0.95 * kept[part] + grads_f
        kept[part] = momentum_next
        nest[part] = (grads_f + 0.95 * momentum_next).astype(jnp.bfloat16)
        return carry

    lax.fori_loop(0, 256 // CHUNK, blend, 0)
    pl.semaphore_wait(barrier, 255)

    own = pltpu.make_async_copy(nest.at[me], whole.at[my_tensor, my_shard], recv_sem)
    own.start()

    def forward(to_x, to_y, to_z, to_core):
        shard, tensor = mesh_index(to_x, to_y, to_z, to_core)
        pltpu.make_async_remote_copy(
            src_ref=nest.at[shard * 4 + tensor],
            dst_ref=whole.at[my_tensor, my_shard],
            send_sem=send_sem,
            recv_sem=recv_sem,
            device_id=(shard, tensor),
            device_id_type=MESH,
        ).start()

    for to_core in (0, 1):

        def to_plane(step, carry, to_core=to_core):
            to_x, to_y = (x + step) % 4, (y + step // 4) % 4
            for hop in HOPS:
                if hop == 0:

                    @pl.when((step > 0) | (core != to_core))
                    def _():
                        forward(to_x, to_y, z, to_core)
                else:
                    forward(to_x, to_y, (z + hop) % 8, to_core)
            return carry

        lax.fori_loop(0, 16, to_plane, 0)

    pltpu.make_async_copy(whole, whole, recv_sem).wait()

    def panel(ref, t, i):
        return ref[t, pl.ds(i * 16, 16)].reshape(256, 256)

    def make_gram(ref, i):
        total = None
        for t in range(4):
            part = dot(panel(ref, t, i), ref[t].reshape(1024, 256), NT)
            total = part if total is None else total + part
        return total

    def rows(i):
        return pl.ds(pl.multiple_of(i * 256, 256), 256)

    def first_gram(i, carry):
        gram_f[rows(i), :] = make_gram(whole, i)
        return carry

    lax.fori_loop(0, 4, first_gram, 0)
    squares = jnp.zeros((256, 256), jnp.float32)
    diagonal = lax.broadcasted_iota(jnp.int32, (256, 256), 0) == lax.broadcasted_iota(jnp.int32, (256, 256), 1)
    for i in range(4):
        squares += jnp.where(diagonal, gram_f[256 * i : 256 * i + 256, 256 * i : 256 * i + 256], 0.0)
    norm = jnp.sqrt(jnp.sum(squares, keepdims=True))
    scale = 1.0 / (norm + 1e-7)

    def round_gram(i, carry):
        gram[rows(i), :] = (gram_f[rows(i), :] * (scale * scale)).astype(jnp.bfloat16)
        return carry

    lax.fori_loop(0, 4, round_gram, 0)

    def make_poly(i, carry):
        strip = gram[rows(i), :]
        poly[rows(i), :] = (B * strip.astype(jnp.float32) + C * dot(strip, gram[...])).astype(jnp.bfloat16)
        return carry

    lax.fori_loop(0, 4, make_poly, 0)

    def first_step(i, carry):
        for t in range(4):
            value = A * panel(whole, t, i).astype(jnp.float32) + dot(poly[rows(i), :], whole[t].reshape(1024, 256))
            mid[t, pl.ds(i * 16, 16)] = (value * scale).astype(jnp.bfloat16).reshape(16, 16, 256)
        return carry

    lax.fori_loop(0, 4, first_step, 0)

    def second_gram(i, carry):
        gram[rows(i), :] = make_gram(mid, i).astype(jnp.bfloat16)
        return carry

    lax.fori_loop(0, 4, second_gram, 0)
    lax.fori_loop(0, 4, make_poly, 0)

    def backward(to_x, to_y, to_z, to_core):
        shard, tensor = mesh_index(to_x, to_y, to_z, to_core)
        pltpu.make_async_remote_copy(
            src_ref=upd.at[tensor, shard],
            dst_ref=out.at[me],
            send_sem=back_send_sem,
            recv_sem=back_recv_sem,
            device_id=(shard, tensor),
            device_id_type=MESH,
        ).start()

    def second_step(step, carry):
        to_y = (y + step) % 4
        for t in range(4):
            value = A * panel(mid, t, to_y).astype(jnp.float32) + dot(poly[rows(to_y), :], mid[t].reshape(1024, 256))
            upd[t, pl.ds(to_y * 16, 16)] = (0.2 * 32.0 * value).astype(jnp.bfloat16).reshape(16, 16, 256)

        def to_line(line, carry):
            to_x, to_core = (x + line // 2) % 4, (core + line) % 2
            for hop in HOPS:
                if hop == 0:

                    @pl.when((step > 0) | (line > 0))
                    def _():
                        backward(to_x, to_y, z, to_core)
                else:
                    backward(to_x, to_y, (z + hop) % 8, to_core)
            return carry

        lax.fori_loop(0, 8, to_line, 0)
        return carry

    lax.fori_loop(0, 4, second_step, 0)
    stay = pltpu.make_async_copy(upd.at[my_tensor, my_shard], out.at[me], back_recv_sem)
    stay.start()

    sent = nest.at[pl.ds(0, 255)]
    pltpu.make_async_copy(sent, sent, send_sem).wait()
    pltpu.make_async_copy(sent, sent, back_send_sem).wait()
    pltpu.make_async_copy(out, out, back_recv_sem).wait()


def write_out(kept, out, kept_hbm, out_hbm, sem):
    copies = [pltpu.make_async_copy(kept, kept_hbm, sem.at[0]), pltpu.make_async_copy(out, out_hbm, sem.at[1])]
    for copy in copies:
        copy.start()
    for copy in copies:
        copy.wait()


def shards(grads, momentum):
    vmem = pl.BlockSpec(memory_space=pltpu.VMEM)
    hbm = pl.BlockSpec(memory_space=pltpu.HBM)
    panels = (4, 64, 16, 256)
    square = (1024, 1024)
    kept, update = pl.pallas_call(
        kernel,
        name="muon",
        out_shape=(pltpu.VMEM(momentum.shape, jnp.float32), pltpu.VMEM(grads.shape, jnp.bfloat16)),
        in_specs=[hbm, hbm],
        out_specs=(vmem, vmem),
        scratch_shapes=[
            pltpu.VMEM(grads.shape, jnp.bfloat16),
            pltpu.VMEM(grads.shape, jnp.bfloat16),
            pltpu.VMEM(panels, jnp.bfloat16),
            pltpu.VMEM(square, jnp.float32),
            pltpu.VMEM(square, jnp.bfloat16),
            pltpu.VMEM(square, jnp.bfloat16),
            pltpu.VMEM(panels, jnp.bfloat16),
            pltpu.VMEM(panels, jnp.bfloat16),
            pltpu.SemaphoreType.DMA((2, 256 // CHUNK)),
            pltpu.SemaphoreType.DMA,
            pltpu.SemaphoreType.DMA,
            pltpu.SemaphoreType.DMA,
            pltpu.SemaphoreType.DMA,
        ],
        compiler_params=pltpu.CompilerParams(collective_id=0, has_side_effects=True, vmem_limit_bytes=57 * 2**20),
    )(grads, momentum)
    return pl.pallas_call(
        write_out,
        name="write_out",
        out_shape=(
            jax.ShapeDtypeStruct(momentum.shape, jnp.float32),
            jax.ShapeDtypeStruct(grads.shape, jnp.bfloat16),
        ),
        in_specs=[vmem, vmem],
        out_specs=(hbm, hbm),
        scratch_shapes=[pltpu.SemaphoreType.DMA((2,))],
        compiler_params=pltpu.CompilerParams(vmem_limit_bytes=2**20),
    )(kept, update)


def solution(mesh):
    spec = P(None, "shard", "tensor")
    return jax.shard_map(shards, mesh=mesh, in_specs=(spec, spec), out_specs=(spec, spec), check_vma=False)
```

```python
import jax
import jax.numpy as jnp
from jax import lax
from jax.experimental import pallas as pl
from jax.experimental.pallas import tpu as pltpu
from jax.sharding import PartitionSpec as P

MESH = pl.DeviceIdType.MESH
NN = (((1,), (0,)), ((), ()))
NT = (((1,), (1,)), ((), ()))
A, B, C = 3.4445, -4.775, 2.0315
EARLY = 5
HOPS = (4, 1, -1, 2, -2, 3, -3, 0)
BACK_HOPS = (4, 3, -3, 2, -2, 0, 1, -1)
OWNERS = (4, 2, 4, 2, 4)


def dot(left, right, dims=NN):
    return lax.dot_general(left, right, dims, preferred_element_type=jnp.float32)


def kernel(grads, momentum, kept, out, fresh, nest, whole, gram_f, gram, poly, mid, upd, load_sem, ready_sem, send_sem, recv_sem, back_send_sem, back_recv_sem):
    my_shard, my_tensor = lax.axis_index("shard"), lax.axis_index("tensor")
    x, y, core = (my_shard // 2) % 4, my_shard // 16, my_shard % 2
    my_low = (my_shard // 8) % 2
    z = my_tensor * 2 + my_low

    def depth(hop):
        to_z = (z + hop) % 8
        return to_z % 2, to_z // 2

    def shard_of(to_x, to_y, low, to_core):
        return to_y * 16 + low * 8 + to_x * 2 + to_core

    def column(step):
        return (x + step % 4) % 4, (y + step // 4) % 4

    def load(step):
        to_x, to_y = column(step)
        return (
            pltpu.make_async_copy(grads.at[to_y, :, to_x], fresh.at[to_y, :, to_x], load_sem.at[0, step]),
            pltpu.make_async_copy(momentum.at[to_y, :, to_x], kept.at[to_y, :, to_x], load_sem.at[1, step]),
        )

    def start_load(step, carry):
        for copy in load(step):
            copy.start()
        return carry

    lax.fori_loop(0, 2, start_load, 0)

    barrier = pltpu.get_barrier_semaphore()
    for hop in (4, 3, -3, 2, -2, 1, -1):
        low, tensor = depth(hop)
        for to_core in (0, 1):
            pl.semaphore_signal(barrier, inc=1, device_id=(shard_of(x, y, low, to_core), tensor), device_id_type=MESH)

    def greet(step, carry):
        to_x, to_y = column(step)
        for to_core in (0, 1):
            pl.semaphore_signal(barrier, inc=1, device_id=(shard_of(to_x, to_y, my_low, to_core), my_tensor), device_id_type=MESH)
        return carry

    lax.fori_loop(1, 16, greet, 0)
    pl.semaphore_signal(barrier, inc=1, device_id=(shard_of(x, y, my_low, 1 - core), my_tensor), device_id_type=MESH)
    lax.fori_loop(2, 16, start_load, 0)

    def blend(step, carry):
        for copy in load(step):
            copy.wait()
        to_x, to_y = column(step)
        for low in (0, 1):
            grads_f = fresh[to_y, low, to_x].astype(jnp.float32)
            momentum_next = 0.95 * kept[to_y, low, to_x] + grads_f
            kept[to_y, low, to_x] = momentum_next
            nest[to_y, low, to_x] = (grads_f + 0.95 * momentum_next).astype(jnp.bfloat16).reshape(2, 4, 16, 256)
        return carry

    def piece(ref, shard, tensor):
        return ref.at[shard, :, pl.ds(pl.multiple_of(tensor * 256, 256), 256)]

    def forward(to_x, to_y, hop, to_core):
        low, tensor = depth(hop)
        shard = shard_of(to_x, to_y, low, to_core)
        pltpu.make_async_remote_copy(
            src_ref=nest.at[to_y, low, to_x, to_core, tensor],
            dst_ref=piece(whole, my_shard, my_tensor),
            send_sem=send_sem,
            recv_sem=recv_sem,
            device_id=(shard, tensor),
            device_id_type=MESH,
        ).start()

    lax.fori_loop(0, 2, blend, 0)
    pl.semaphore_wait(barrier, 45)
    for hop in (4, 3, -3, 2, -2, 1, -1):
        low, tensor = depth(hop)
        pl.semaphore_signal(ready_sem, inc=1, device_id=(shard_of(x, y, low, core), tensor), device_id_type=MESH)

    for to_core in (0, 1):
        for hop in HOPS:
            if hop != 0:
                forward(x, y, hop, to_core)
    forward(x, y, 0, 1 - core)
    own = pltpu.make_async_copy(nest.at[y, my_low, x, core, my_tensor], piece(whole, my_shard, my_tensor), recv_sem)
    own.start()
    lax.fori_loop(2, EARLY + 1, blend, 0)
    pl.semaphore_wait(ready_sem, 7)

    def to_column(to_core, blending):
        def body(step, carry):
            to_x, to_y = column(step)
            for hop in HOPS:
                forward(to_x, to_y, hop, to_core)
            if blending:
                blend(step + EARLY, carry)
            return carry

        return body

    lax.fori_loop(1, 16 - EARLY, to_column(0, True), 0)
    lax.fori_loop(16 - EARLY, 16, to_column(0, False), 0)
    lax.fori_loop(1, 16, to_column(1, False), 0)
    pltpu.make_async_copy(whole, whole, recv_sem).wait()

    def rows(i):
        return pl.ds(pl.multiple_of(i * 256, 256), 256)

    def strip(ref, i):
        return ref[pl.ds(i * 16, 16)].reshape(256, 1024)

    def square(ref):
        return ref[...].reshape(1024, 1024)

    def first_gram(i, carry):
        gram_f[rows(i), :] = dot(strip(whole, i), square(whole), NT)
        return carry

    lax.fori_loop(0, 4, first_gram, 0)
    squares = jnp.zeros((256, 256), jnp.float32)
    diagonal = lax.broadcasted_iota(jnp.int32, (256, 256), 0) == lax.broadcasted_iota(jnp.int32, (256, 256), 1)
    for i in range(4):
        squares += jnp.where(diagonal, gram_f[256 * i : 256 * i + 256, 256 * i : 256 * i + 256], 0.0)
    norm = jnp.sqrt(jnp.sum(squares, keepdims=True))
    scale = 1.0 / (norm + 1e-7)

    def round_gram(i, carry):
        gram[rows(i), :] = (gram_f[rows(i), :] * (scale * scale)).astype(jnp.bfloat16)
        return carry

    lax.fori_loop(0, 4, round_gram, 0)

    def make_poly(i, carry):
        part = gram[rows(i), :]
        poly[rows(i), :] = (B * part.astype(jnp.float32) + C * dot(part, gram[...])).astype(jnp.bfloat16)
        return carry

    lax.fori_loop(0, 4, make_poly, 0)

    def first_step(i, carry):
        value = A * strip(whole, i).astype(jnp.float32) + dot(poly[rows(i), :], square(whole))
        mid[pl.ds(i * 16, 16)] = (value * scale).astype(jnp.bfloat16).reshape(16, 16, 1024)
        return carry

    lax.fori_loop(0, 4, first_step, 0)

    def second_gram(i, carry):
        gram[rows(i), :] = dot(strip(mid, i), square(mid), NT).astype(jnp.bfloat16)
        return carry

    lax.fori_loop(0, 4, second_gram, 0)
    lax.fori_loop(0, 4, make_poly, 0)

    def backward(to_x, to_y, hop, to_core):
        low, tensor = depth(hop)
        shard = shard_of(to_x, to_y, low, to_core)
        pltpu.make_async_remote_copy(
            src_ref=piece(upd, shard, tensor),
            dst_ref=out.at[y, my_low, x, core, my_tensor],
            send_sem=back_send_sem,
            recv_sem=back_recv_sem,
            device_id=(shard, tensor),
            device_id_type=MESH,
        ).start()

    def second_step(step, carry):
        to_y = (y + step) % 4
        value = A * strip(mid, to_y).astype(jnp.float32) + dot(poly[rows(to_y), :], square(mid))
        upd[pl.ds(to_y * 16, 16)] = (0.2 * 32.0 * value).astype(jnp.bfloat16).reshape(16, 16, 1024)
        return carry

    def send_strip(step):
        to_y = (y + step) % 4
        for hop in BACK_HOPS:

            def to_line(line, carry, hop=hop):
                to_x, to_core = (x + line // 2) % 4, (core + line) % 2
                if hop == 0:

                    @pl.when((step > 0) | (line > 0))
                    def _():
                        backward(to_x, to_y, hop, to_core)
                else:
                    backward(to_x, to_y, hop, to_core)
                return carry

            lax.fori_loop(0, 8, to_line, 0)

    def step_and_send(step, carry):
        second_step(step, carry)
        send_strip(step)
        return carry

    lax.fori_loop(0, 4, step_and_send, 0)
    stay = pltpu.make_async_copy(piece(upd, my_shard, my_tensor), out.at[y, my_low, x, core, my_tensor], back_recv_sem)
    stay.start()

    sent = whole.at[pl.ds(0, 63)]
    rest = piece(whole, 0, 0)
    for sem in (send_sem, back_send_sem):
        pltpu.make_async_copy(sent, sent, sem).wait()
        for _ in range(3):
            pltpu.make_async_copy(rest, rest, sem).wait()
    pltpu.make_async_copy(out, out, back_recv_sem).wait()


def write_out(kept, out, kept_hbm, out_hbm, sem):
    copies = [pltpu.make_async_copy(kept, kept_hbm, sem.at[0]), pltpu.make_async_copy(out, out_hbm, sem.at[1])]
    for copy in copies:
        copy.start()
    for copy in copies:
        copy.wait()


def shards(grads, momentum):
    vmem = pl.BlockSpec(memory_space=pltpu.VMEM)
    hbm = pl.BlockSpec(memory_space=pltpu.HBM)
    piece = grads.shape[1:]
    by_column = OWNERS[:3] + (8,) + piece
    by_owner = OWNERS + piece
    block = (64, 16, 1024)
    square = (1024, 1024)
    kept, update = pl.pallas_call(
        kernel,
        name="muon",
        out_shape=(pltpu.VMEM(by_column, jnp.float32), pltpu.VMEM(by_owner, jnp.bfloat16)),
        in_specs=[hbm, hbm],
        out_specs=(vmem, vmem),
        scratch_shapes=[
            pltpu.VMEM(by_column, jnp.bfloat16),
            pltpu.VMEM(by_owner, jnp.bfloat16),
            pltpu.VMEM(block, jnp.bfloat16),
            pltpu.VMEM(square, jnp.float32),
            pltpu.VMEM(square, jnp.bfloat16),
            pltpu.VMEM(square, jnp.bfloat16),
            pltpu.VMEM(block, jnp.bfloat16),
            pltpu.VMEM(block, jnp.bfloat16),
            pltpu.SemaphoreType.DMA((2, 16)),
            pltpu.SemaphoreType.REGULAR,
            pltpu.SemaphoreType.DMA,
            pltpu.SemaphoreType.DMA,
            pltpu.SemaphoreType.DMA,
            pltpu.SemaphoreType.DMA,
        ],
        compiler_params=pltpu.CompilerParams(collective_id=0, has_side_effects=True, vmem_limit_bytes=57 * 2**20),
    )(grads.reshape(by_column), momentum.reshape(by_column))
    return pl.pallas_call(
        write_out,
        name="write_out",
        out_shape=(
            jax.ShapeDtypeStruct(momentum.shape, jnp.float32),
            jax.ShapeDtypeStruct(grads.shape, jnp.bfloat16),
        ),
        in_specs=[vmem, vmem],
        out_specs=(hbm, hbm),
        scratch_shapes=[pltpu.SemaphoreType.DMA((2,))],
        compiler_params=pltpu.CompilerParams(vmem_limit_bytes=2**20),
    )(kept.reshape(momentum.shape), update.reshape(grads.shape))


def solution(mesh):
    spec = P(None, "shard", "tensor")
    return jax.shard_map(shards, mesh=mesh, in_specs=(spec, spec), out_specs=(spec, spec), check_vma=False)
```

```python
import jax
import jax.numpy as jnp
from jax import lax
from jax.experimental import pallas as pl
from jax.experimental.pallas import tpu as pltpu
from jax.sharding import PartitionSpec as P

MESH = pl.DeviceIdType.MESH
NN = (((1,), (0,)), ((), ()))
NT = (((1,), (1,)), ((), ()))
A, B, C = 3.4445, -4.775, 2.0315
EARLY = 5
HOPS = (4, 1, -1, 2, -2, 3, -3, 0)
OWNERS = (4, 2, 4, 2, 4)


def dot(left, right, dims=NN):
    return lax.dot_general(left, right, dims, preferred_element_type=jnp.float32)


def kernel(grads, momentum, kept, out, fresh, nest, whole, gram, poly, mid, upd, load_sem, ready_sem, send_sem, recv_sem, back_send_sem, back_recv_sem):
    my_shard, my_tensor = lax.axis_index("shard"), lax.axis_index("tensor")
    x, y, core = (my_shard // 2) % 4, my_shard // 16, my_shard % 2
    my_low = (my_shard // 8) % 2
    z = my_tensor * 2 + my_low

    def depth(hop):
        to_z = (z + hop) % 8
        return to_z % 2, to_z // 2

    def shard_of(to_x, to_y, low, to_core):
        return to_y * 16 + low * 8 + to_x * 2 + to_core

    def column(step):
        return (x + step % 4) % 4, (y + step // 4) % 4

    def load(step):
        to_x, to_y = column(step)
        return (
            pltpu.make_async_copy(grads.at[to_y, :, to_x], fresh.at[to_y, :, to_x], load_sem.at[0, step]),
            pltpu.make_async_copy(momentum.at[to_y, :, to_x], kept.at[to_y, :, to_x], load_sem.at[1, step]),
        )

    def start_load(step, carry):
        for copy in load(step):
            copy.start()
        return carry

    lax.fori_loop(0, 2, start_load, 0)

    barrier = pltpu.get_barrier_semaphore()
    for hop in (4, 3, -3, 2, -2, 1, -1):
        low, tensor = depth(hop)
        for to_core in (0, 1):
            pl.semaphore_signal(barrier, inc=1, device_id=(shard_of(x, y, low, to_core), tensor), device_id_type=MESH)

    def greet(step, carry):
        to_x, to_y = column(step)
        for to_core in (0, 1):
            pl.semaphore_signal(barrier, inc=1, device_id=(shard_of(to_x, to_y, my_low, to_core), my_tensor), device_id_type=MESH)
        return carry

    lax.fori_loop(1, 16, greet, 0)
    pl.semaphore_signal(barrier, inc=1, device_id=(shard_of(x, y, my_low, 1 - core), my_tensor), device_id_type=MESH)
    lax.fori_loop(2, 16, start_load, 0)

    def blend(step, carry):
        for copy in load(step):
            copy.wait()
        to_x, to_y = column(step)
        for low in (0, 1):
            grads_f = fresh[to_y, low, to_x].astype(jnp.float32)
            momentum_next = 0.95 * kept[to_y, low, to_x] + grads_f
            kept[to_y, low, to_x] = momentum_next
            nest[to_y, low, to_x] = (grads_f + 0.95 * momentum_next).astype(jnp.bfloat16).reshape(2, 4, 16, 256)
        return carry

    def piece(ref, shard, tensor):
        return ref.at[shard, :, pl.ds(pl.multiple_of(tensor * 256, 256), 256)]

    def forward(to_x, to_y, hop, to_core):
        low, tensor = depth(hop)
        shard = shard_of(to_x, to_y, low, to_core)
        pltpu.make_async_remote_copy(
            src_ref=nest.at[to_y, low, to_x, to_core, tensor],
            dst_ref=piece(whole, my_shard, my_tensor),
            send_sem=send_sem,
            recv_sem=recv_sem,
            device_id=(shard, tensor),
            device_id_type=MESH,
        ).start()

    lax.fori_loop(0, 2, blend, 0)
    pl.semaphore_wait(barrier, 45)
    for hop in (4, 3, -3, 2, -2, 1, -1):
        low, tensor = depth(hop)
        pl.semaphore_signal(ready_sem, inc=1, device_id=(shard_of(x, y, low, core), tensor), device_id_type=MESH)

    for to_core in (0, 1):
        for hop in HOPS:
            if hop != 0:
                forward(x, y, hop, to_core)
    forward(x, y, 0, 1 - core)
    own = pltpu.make_async_copy(nest.at[y, my_low, x, core, my_tensor], piece(whole, my_shard, my_tensor), recv_sem)
    own.start()
    lax.fori_loop(2, EARLY + 1, blend, 0)
    pl.semaphore_wait(ready_sem, 7)

    def to_column(to_core, blending):
        def body(step, carry):
            to_x, to_y = column(step)
            for hop in HOPS:
                forward(to_x, to_y, hop, to_core)
            if blending:
                blend(step + EARLY, carry)
            return carry

        return body

    lax.fori_loop(1, 16 - EARLY, to_column(0, True), 0)
    lax.fori_loop(16 - EARLY, 16, to_column(0, False), 0)
    lax.fori_loop(1, 16, to_column(1, False), 0)
    pltpu.make_async_copy(whole, whole, recv_sem).wait()

    def columns(j):
        return pl.ds(pl.multiple_of(j * 256, 256), 256)

    def strip(ref, i):
        return ref[pl.ds(i * 16, 16)].reshape(256, 1024)

    def panel(ref, j):
        return ref[:, :, columns(j)].reshape(1024, 256)

    def square(ref):
        return ref[...].reshape(1024, 1024)

    def add_squares(i, total):
        part = strip(whole, i).astype(jnp.float32)
        return total + jnp.sum((part * part).reshape(32, 8, 1024), axis=0)

    total = lax.fori_loop(0, 4, add_squares, jnp.zeros((8, 1024), jnp.float32))
    scale = 1.0 / (jnp.sqrt(jnp.sum(total, keepdims=True)) + 1e-7)

    def first_gram(j, carry):
        gram[:, columns(j)] = (dot(square(whole), strip(whole, j), NT) * (scale * scale)).astype(jnp.bfloat16)
        return carry

    def make_poly(j, carry):
        part = gram[:, columns(j)]
        poly[:, columns(j)] = (B * part.astype(jnp.float32) + C * dot(gram[...], part)).astype(jnp.bfloat16)
        return carry

    def first_step(j, carry):
        part = panel(whole, j)
        value = A * part.astype(jnp.float32) + dot(poly[...], part)
        mid[:, :, columns(j)] = (value * scale).astype(jnp.bfloat16).reshape(64, 16, 256)
        return carry

    def second_gram(j, carry):
        gram[:, columns(j)] = dot(square(mid), strip(mid, j), NT).astype(jnp.bfloat16)
        return carry

    for body in (first_gram, make_poly, first_step, second_gram, make_poly):
        lax.fori_loop(0, 4, body, 0)

    def second_step(tensor):
        part = panel(mid, tensor)
        value = A * part.astype(jnp.float32) + dot(poly[...], part)
        upd[tensor] = (0.2 * 32.0 * value).astype(jnp.bfloat16).reshape(64, 16, 256)

    def send_panel(tensor):
        def to_line(line, carry):
            to_x, to_y = (x + line // 2) % 4, (y + line // 8) % 4
            for other in (1, 0):
                shard = shard_of(to_x, to_y, (my_low + other) % 2, (core + line) % 2)

                @pl.when((shard != my_shard) | (tensor != my_tensor))
                def _():
                    pltpu.make_async_remote_copy(
                        src_ref=upd.at[tensor, shard],
                        dst_ref=out.at[y, my_low, x, core, my_tensor],
                        send_sem=back_send_sem,
                        recv_sem=back_recv_sem,
                        device_id=(shard, tensor),
                        device_id_type=MESH,
                    ).start()
            return carry

        lax.fori_loop(0, 32, to_line, 0)

    def step_and_send(step, carry):
        tensor = (my_tensor + 2 + step) % 4
        second_step(tensor)
        send_panel(tensor)
        return carry

    lax.fori_loop(0, 4, step_and_send, 0)
    stay = pltpu.make_async_copy(upd.at[my_tensor, my_shard], out.at[y, my_low, x, core, my_tensor], back_recv_sem)
    stay.start()

    sent = whole.at[pl.ds(0, 63)]
    rest = piece(whole, 0, 0)
    for sem in (send_sem, back_send_sem):
        pltpu.make_async_copy(sent, sent, sem).wait()
        for _ in range(3):
            pltpu.make_async_copy(rest, rest, sem).wait()
    pltpu.make_async_copy(out, out, back_recv_sem).wait()


def write_out(kept, out, kept_hbm, out_hbm, sem):
    copies = [pltpu.make_async_copy(kept, kept_hbm, sem.at[0]), pltpu.make_async_copy(out, out_hbm, sem.at[1])]
    for copy in copies:
        copy.start()
    for copy in copies:
        copy.wait()


def shards(grads, momentum):
    vmem = pl.BlockSpec(memory_space=pltpu.VMEM)
    hbm = pl.BlockSpec(memory_space=pltpu.HBM)
    piece = grads.shape[1:]
    by_column = OWNERS[:3] + (8,) + piece
    by_owner = OWNERS + piece
    block = (64, 16, 1024)
    square = (1024, 1024)
    kept, update = pl.pallas_call(
        kernel,
        name="muon",
        out_shape=(pltpu.VMEM(by_column, jnp.float32), pltpu.VMEM(by_owner, jnp.bfloat16)),
        in_specs=[hbm, hbm],
        out_specs=(vmem, vmem),
        scratch_shapes=[
            pltpu.VMEM(by_column, jnp.bfloat16),
            pltpu.VMEM(by_owner, jnp.bfloat16),
            pltpu.VMEM(block, jnp.bfloat16),
            pltpu.VMEM(square, jnp.bfloat16),
            pltpu.VMEM(square, jnp.bfloat16),
            pltpu.VMEM(block, jnp.bfloat16),
            pltpu.VMEM((4, 64, 16, 256), jnp.bfloat16),
            pltpu.SemaphoreType.DMA((2, 16)),
            pltpu.SemaphoreType.REGULAR,
            pltpu.SemaphoreType.DMA,
            pltpu.SemaphoreType.DMA,
            pltpu.SemaphoreType.DMA,
            pltpu.SemaphoreType.DMA,
        ],
        compiler_params=pltpu.CompilerParams(collective_id=0, has_side_effects=True, vmem_limit_bytes=57 * 2**20),
    )(grads.reshape(by_column), momentum.reshape(by_column))
    return pl.pallas_call(
        write_out,
        name="write_out",
        out_shape=(
            jax.ShapeDtypeStruct(momentum.shape, jnp.float32),
            jax.ShapeDtypeStruct(grads.shape, jnp.bfloat16),
        ),
        in_specs=[vmem, vmem],
        out_specs=(hbm, hbm),
        scratch_shapes=[pltpu.SemaphoreType.DMA((2,))],
        compiler_params=pltpu.CompilerParams(vmem_limit_bytes=2**20),
    )(kept.reshape(momentum.shape), update.reshape(grads.shape))


def solution(mesh):
    spec = P(None, "shard", "tensor")
    return jax.shard_map(shards, mesh=mesh, in_specs=(spec, spec), out_specs=(spec, spec), check_vma=False)
```

```python
import jax
import jax.numpy as jnp
from jax import lax
from jax.experimental import pallas as pl
from jax.experimental.pallas import tpu as pltpu
from jax.sharding import PartitionSpec as P

MESH = pl.DeviceIdType.MESH
NN = (((1,), (0,)), ((), ()))
NT = (((1,), (1,)), ((), ()))
A, B, C = 3.4445, -4.775, 2.0315
EARLY = 5
HOPS = (4, 1, -1, 2, -2, 3, -3, 0)
PARTS = 8
OWNERS = (4, 2, 4, 2, 4)


def dot(left, right, dims=NN):
    return lax.dot_general(left, right, dims, preferred_element_type=jnp.float32)


def kernel(grads, momentum, kept, out, fresh, nest, whole, gram, poly, mid, upd, load_sem, ready_sem, send_sem, recv_sem, back_send_sem, back_recv_sem):
    my_shard, my_tensor = lax.axis_index("shard"), lax.axis_index("tensor")
    x, y, core = (my_shard // 2) % 4, my_shard // 16, my_shard % 2
    my_low = (my_shard // 8) % 2
    z = my_tensor * 2 + my_low

    def depth(hop):
        to_z = (z + hop) % 8
        return to_z % 2, to_z // 2

    def shard_of(to_x, to_y, low, to_core):
        return to_y * 16 + low * 8 + to_x * 2 + to_core

    def column(step):
        return (x + step % 4) % 4, (y + step // 4) % 4

    def load(step):
        to_x, to_y = column(step)
        return (
            pltpu.make_async_copy(grads.at[to_y, :, to_x], fresh.at[to_y, :, to_x], load_sem.at[0, step]),
            pltpu.make_async_copy(momentum.at[to_y, :, to_x], kept.at[to_y, :, to_x], load_sem.at[1, step]),
        )

    def start_load(step, carry):
        for copy in load(step):
            copy.start()
        return carry

    lax.fori_loop(0, 2, start_load, 0)

    barrier = pltpu.get_barrier_semaphore()
    for hop in (4, 3, -3, 2, -2, 1, -1):
        low, tensor = depth(hop)
        for to_core in (0, 1):
            pl.semaphore_signal(barrier, inc=1, device_id=(shard_of(x, y, low, to_core), tensor), device_id_type=MESH)

    def greet(step, carry):
        to_x, to_y = (x + 2 + step % 4) % 4, (y + 2 + step // 4) % 4

        @pl.when(step != 10)
        def _():
            for to_core in (0, 1):
                pl.semaphore_signal(barrier, inc=1, device_id=(shard_of(to_x, to_y, my_low, to_core), my_tensor), device_id_type=MESH)

        return carry

    lax.fori_loop(0, 16, greet, 0)
    pl.semaphore_signal(barrier, inc=1, device_id=(shard_of(x, y, my_low, 1 - core), my_tensor), device_id_type=MESH)
    lax.fori_loop(2, 16, start_load, 0)

    def blend(step, carry):
        for copy in load(step):
            copy.wait()
        to_x, to_y = column(step)
        for low in (0, 1):
            grads_f = fresh[to_y, low, to_x].astype(jnp.float32)
            momentum_next = 0.95 * kept[to_y, low, to_x] + grads_f
            kept[to_y, low, to_x] = momentum_next
            nest[to_y, low, to_x] = (grads_f + 0.95 * momentum_next).astype(jnp.bfloat16).reshape(2, 4, 16, 256)
        return carry

    def piece(ref, shard, tensor):
        return ref.at[shard, :, pl.ds(pl.multiple_of(tensor * 256, 256), 256)]

    def forward(to_x, to_y, hop, to_core):
        low, tensor = depth(hop)
        shard = shard_of(to_x, to_y, low, to_core)
        pltpu.make_async_remote_copy(
            src_ref=nest.at[to_y, low, to_x, to_core, tensor],
            dst_ref=piece(whole, my_shard, my_tensor),
            send_sem=send_sem,
            recv_sem=recv_sem,
            device_id=(shard, tensor),
            device_id_type=MESH,
        ).start()

    lax.fori_loop(0, 2, blend, 0)
    pl.semaphore_wait(barrier, 45)
    for hop in (4, 3, -3, 2, -2, 1, -1):
        low, tensor = depth(hop)
        pl.semaphore_signal(ready_sem, inc=1, device_id=(shard_of(x, y, low, core), tensor), device_id_type=MESH)

    for to_core in (0, 1):
        for hop in HOPS:
            if hop != 0:
                forward(x, y, hop, to_core)
    forward(x, y, 0, 1 - core)
    own = pltpu.make_async_copy(nest.at[y, my_low, x, core, my_tensor], piece(whole, my_shard, my_tensor), recv_sem)
    own.start()
    lax.fori_loop(2, EARLY + 1, blend, 0)
    pl.semaphore_wait(ready_sem, 7)

    def to_column(to_core, blending):
        def body(step, carry):
            to_x, to_y = column(step)
            for hop in HOPS:
                forward(to_x, to_y, hop, to_core)
            if blending:
                blend(step + EARLY, carry)
            return carry

        return body

    lax.fori_loop(1, 16 - EARLY, to_column(0, True), 0)
    lax.fori_loop(16 - EARLY, 16, to_column(0, False), 0)
    lax.fori_loop(1, 16, to_column(1, False), 0)
    pltpu.make_async_copy(whole, whole, recv_sem).wait()

    def columns(j):
        return pl.ds(pl.multiple_of(j * 256, 256), 256)

    def strip(ref, i):
        return ref[pl.ds(i * 16, 16)].reshape(256, 1024)

    def panel(ref, j):
        return ref[:, :, columns(j)].reshape(1024, 256)

    def square(ref):
        return ref[...].reshape(1024, 1024)

    def add_squares(i, total):
        part = strip(whole, i).astype(jnp.float32)
        return total + jnp.sum((part * part).reshape(32, 8, 1024), axis=0)

    total = lax.fori_loop(0, 4, add_squares, jnp.zeros((8, 1024), jnp.float32))
    scale = 1.0 / (jnp.sqrt(jnp.sum(total, keepdims=True)) + 1e-7)

    def first_gram(j, carry):
        gram[:, columns(j)] = (dot(square(whole), strip(whole, j), NT) * (scale * scale)).astype(jnp.bfloat16)
        return carry

    def make_poly(j, carry):
        part = gram[:, columns(j)]
        poly[:, columns(j)] = (B * part.astype(jnp.float32) + C * dot(gram[...], part)).astype(jnp.bfloat16)
        return carry

    def first_step(j, carry):
        part = panel(whole, j)
        value = A * part.astype(jnp.float32) + dot(poly[...], part)
        mid[:, :, columns(j)] = (value * scale).astype(jnp.bfloat16).reshape(64, 16, 256)
        return carry

    def second_gram(j, carry):
        gram[:, columns(j)] = dot(square(mid), strip(mid, j), NT).astype(jnp.bfloat16)
        return carry

    for body in (first_gram, make_poly, first_step, second_gram, make_poly):
        lax.fori_loop(0, 4, body, 0)

    def second_step(tensor):
        part = panel(mid, tensor)
        value = A * part.astype(jnp.float32) + dot(poly[...], part)
        upd[tensor] = (0.2 * 32.0 * value).astype(jnp.bfloat16).reshape(64, 16, 256)

    def send_panel(tensor):
        def to_line(line, carry):
            to_x, to_y = (x + line // 2) % 4, (y + line // 8) % 4
            for other in (1, 0):
                shard = shard_of(to_x, to_y, (my_low + other) % 2, (core + line) % 2)

                @pl.when((shard != my_shard) | (tensor != my_tensor))
                def _():
                    pltpu.make_async_remote_copy(
                        src_ref=upd.at[tensor, shard],
                        dst_ref=out.at[y, my_low, x, core, my_tensor],
                        send_sem=back_send_sem,
                        recv_sem=back_recv_sem,
                        device_id=(shard, tensor),
                        device_id_type=MESH,
                    ).start()
            return carry

        lax.fori_loop(0, 32, to_line, 0)

    def step_and_send(step, carry):
        tensor = (my_tensor + 2 + step) % 4
        second_step(tensor)
        send_panel(tensor)
        return carry

    lax.fori_loop(0, 4, step_and_send, 0)
    stay = pltpu.make_async_copy(upd.at[my_tensor, my_shard], out.at[y, my_low, x, core, my_tensor], back_recv_sem)
    stay.start()

    sent = whole.at[pl.ds(0, 63)]
    rest = piece(whole, 0, 0)
    for sem in (send_sem, back_send_sem):
        pltpu.make_async_copy(sent, sent, sem).wait()
        for _ in range(3):
            pltpu.make_async_copy(rest, rest, sem).wait()
    pltpu.make_async_copy(out, out, back_recv_sem).wait()


def write_out(kept, out, kept_hbm, out_hbm, sem):
    copies = []
    for i in range(PARTS):
        part = pl.ds(i * (256 // PARTS), 256 // PARTS)
        copies.append(pltpu.make_async_copy(kept.at[part], kept_hbm.at[part], sem.at[0, i]))
        copies.append(pltpu.make_async_copy(out.at[part], out_hbm.at[part], sem.at[1, i]))
    for copy in copies:
        copy.start()
    for copy in copies:
        copy.wait()


def shards(grads, momentum):
    vmem = pl.BlockSpec(memory_space=pltpu.VMEM)
    hbm = pl.BlockSpec(memory_space=pltpu.HBM)
    piece = grads.shape[1:]
    by_column = OWNERS[:3] + (8,) + piece
    by_owner = OWNERS + piece
    block = (64, 16, 1024)
    square = (1024, 1024)
    kept, update = pl.pallas_call(
        kernel,
        name="muon",
        out_shape=(pltpu.VMEM(by_column, jnp.float32), pltpu.VMEM(by_owner, jnp.bfloat16)),
        in_specs=[hbm, hbm],
        out_specs=(vmem, vmem),
        scratch_shapes=[
            pltpu.VMEM(by_column, jnp.bfloat16),
            pltpu.VMEM(by_owner, jnp.bfloat16),
            pltpu.VMEM(block, jnp.bfloat16),
            pltpu.VMEM(square, jnp.bfloat16),
            pltpu.VMEM(square, jnp.bfloat16),
            pltpu.VMEM(block, jnp.bfloat16),
            pltpu.VMEM((4, 64, 16, 256), jnp.bfloat16),
            pltpu.SemaphoreType.DMA((2, 16)),
            pltpu.SemaphoreType.REGULAR,
            pltpu.SemaphoreType.DMA,
            pltpu.SemaphoreType.DMA,
            pltpu.SemaphoreType.DMA,
            pltpu.SemaphoreType.DMA,
        ],
        compiler_params=pltpu.CompilerParams(collective_id=0, has_side_effects=True, vmem_limit_bytes=57 * 2**20),
    )(grads.reshape(by_column), momentum.reshape(by_column))
    return pl.pallas_call(
        write_out,
        name="write_out",
        out_shape=(
            jax.ShapeDtypeStruct(momentum.shape, jnp.float32),
            jax.ShapeDtypeStruct(grads.shape, jnp.bfloat16),
        ),
        in_specs=[vmem, vmem],
        out_specs=(hbm, hbm),
        scratch_shapes=[pltpu.SemaphoreType.DMA((2, PARTS))],
        compiler_params=pltpu.CompilerParams(vmem_limit_bytes=2**20),
    )(kept.reshape(momentum.shape), update.reshape(grads.shape))


def solution(mesh):
    spec = P(None, "shard", "tensor")
    return jax.shard_map(shards, mesh=mesh, in_specs=(spec, spec), out_specs=(spec, spec), check_vma=False)
```

```python
import jax
import jax.numpy as jnp
from jax import lax
from jax.experimental import pallas as pl
from jax.experimental.pallas import tpu as pltpu
from jax.sharding import PartitionSpec as P

MESH = pl.DeviceIdType.MESH
NN = (((1,), (0,)), ((), ()))
NT = (((1,), (1,)), ((), ()))
A, B, C = 3.4445, -4.775, 2.0315
EARLY = 5
HOPS = (4, 1, -1, 2, -2, 3, -3, 0)
OWNERS = (4, 2, 4, 2, 4)


def dot(left, right, dims=NN):
    return lax.dot_general(left, right, dims, preferred_element_type=jnp.float32)


def kernel(grads, momentum, kept, out, fresh, nest, whole, gram, poly, mid, upd, load_sem, ready_sem, send_sem, recv_sem, back_send_sem, back_recv_sem):
    my_shard, my_tensor = lax.axis_index("shard"), lax.axis_index("tensor")
    x, y, core = (my_shard // 2) % 4, my_shard // 16, my_shard % 2
    my_low = (my_shard // 8) % 2
    z = my_tensor * 2 + my_low

    def depth(hop):
        to_z = (z + hop) % 8
        return to_z % 2, to_z // 2

    def shard_of(to_x, to_y, low, to_core):
        return to_y * 16 + low * 8 + to_x * 2 + to_core

    def column(step):
        return (x + step % 4) % 4, (y + step // 4) % 4

    def load(plane):
        to_y = (y + plane) % 4
        return (
            pltpu.make_async_copy(grads.at[to_y], fresh.at[to_y], load_sem.at[0, plane]),
            pltpu.make_async_copy(momentum.at[to_y], kept.at[to_y], load_sem.at[1, plane]),
        )

    for plane in range(4):
        for copy in load(plane):
            copy.start()

    barrier = pltpu.get_barrier_semaphore()
    for hop in (4, 3, -3, 2, -2, 1, -1):
        low, tensor = depth(hop)
        for to_core in (0, 1):
            pl.semaphore_signal(barrier, inc=1, device_id=(shard_of(x, y, low, to_core), tensor), device_id_type=MESH)

    def greet(step, carry):
        to_x, to_y = (x + 2 + step % 4) % 4, (y + 2 + step // 4) % 4

        @pl.when(step != 10)
        def _():
            for to_core in (0, 1):
                pl.semaphore_signal(barrier, inc=1, device_id=(shard_of(to_x, to_y, my_low, to_core), my_tensor), device_id_type=MESH)

        return carry

    lax.fori_loop(0, 16, greet, 0)
    pl.semaphore_signal(barrier, inc=1, device_id=(shard_of(x, y, my_low, 1 - core), my_tensor), device_id_type=MESH)

    def blend(step, carry):
        @pl.when(step % 4 == 0)
        def _():
            for copy in load(step // 4):
                copy.wait()

        to_x, to_y = column(step)
        for low in (0, 1):
            grads_f = fresh[to_y, low, to_x].astype(jnp.float32)
            momentum_next = 0.95 * kept[to_y, low, to_x] + grads_f
            kept[to_y, low, to_x] = momentum_next
            nest[to_y, low, to_x] = (grads_f + 0.95 * momentum_next).astype(jnp.bfloat16).reshape(2, 4, 16, 256)
        return carry

    def piece(ref, shard, tensor):
        return ref.at[shard, :, pl.ds(pl.multiple_of(tensor * 256, 256), 256)]

    def forward(to_x, to_y, hop, to_core):
        low, tensor = depth(hop)
        shard = shard_of(to_x, to_y, low, to_core)
        pltpu.make_async_remote_copy(
            src_ref=nest.at[to_y, low, to_x, to_core, tensor],
            dst_ref=piece(whole, my_shard, my_tensor),
            send_sem=send_sem,
            recv_sem=recv_sem,
            device_id=(shard, tensor),
            device_id_type=MESH,
        ).start()

    lax.fori_loop(0, 2, blend, 0)
    pl.semaphore_wait(barrier, 45)
    for hop in (4, 3, -3, 2, -2, 1, -1):
        low, tensor = depth(hop)
        pl.semaphore_signal(ready_sem, inc=1, device_id=(shard_of(x, y, low, core), tensor), device_id_type=MESH)

    for to_core in (0, 1):
        for hop in HOPS:
            if hop != 0:
                forward(x, y, hop, to_core)
    forward(x, y, 0, 1 - core)
    own = pltpu.make_async_copy(nest.at[y, my_low, x, core, my_tensor], piece(whole, my_shard, my_tensor), recv_sem)
    own.start()
    lax.fori_loop(2, EARLY + 1, blend, 0)
    pl.semaphore_wait(ready_sem, 7)

    def to_column(to_core, blending):
        def body(step, carry):
            to_x, to_y = column(step)
            for hop in HOPS:
                forward(to_x, to_y, hop, to_core)
            if blending:
                blend(step + EARLY, carry)
            return carry

        return body

    lax.fori_loop(1, 16 - EARLY, to_column(0, True), 0)
    lax.fori_loop(16 - EARLY, 16, to_column(0, False), 0)
    lax.fori_loop(1, 16, to_column(1, False), 0)
    pltpu.make_async_copy(whole, whole, recv_sem).wait()

    def columns(j):
        return pl.ds(pl.multiple_of(j * 256, 256), 256)

    def strip(ref, i):
        return ref[pl.ds(i * 16, 16)].reshape(256, 1024)

    def panel(ref, j):
        return ref[:, :, columns(j)].reshape(1024, 256)

    def square(ref):
        return ref[...].reshape(1024, 1024)

    def add_squares(i, total):
        part = strip(whole, i).astype(jnp.float32)
        return total + jnp.sum((part * part).reshape(32, 8, 1024), axis=0)

    total = lax.fori_loop(0, 4, add_squares, jnp.zeros((8, 1024), jnp.float32))
    scale = 1.0 / (jnp.sqrt(jnp.sum(total, keepdims=True)) + 1e-7)

    def first_gram(j, carry):
        gram[:, columns(j)] = (dot(square(whole), strip(whole, j), NT) * (scale * scale)).astype(jnp.bfloat16)
        return carry

    def make_poly(j, carry):
        part = gram[:, columns(j)]
        poly[:, columns(j)] = (B * part.astype(jnp.float32) + C * dot(gram[...], part)).astype(jnp.bfloat16)
        return carry

    def first_step(j, carry):
        part = panel(whole, j)
        value = A * part.astype(jnp.float32) + dot(poly[...], part)
        mid[:, :, columns(j)] = (value * scale).astype(jnp.bfloat16).reshape(64, 16, 256)
        return carry

    def second_gram(j, carry):
        gram[:, columns(j)] = dot(square(mid), strip(mid, j), NT).astype(jnp.bfloat16)
        return carry

    for body in (first_gram, make_poly, first_step, second_gram, make_poly):
        lax.fori_loop(0, 4, body, 0)

    def second_step(tensor):
        part = panel(mid, tensor)
        value = A * part.astype(jnp.float32) + dot(poly[...], part)
        upd[tensor] = (0.2 * 32.0 * value).astype(jnp.bfloat16).reshape(64, 16, 256)

    def send_panel(tensor):
        def to_line(line, carry):
            to_x, to_y = (x + line // 2) % 4, (y + line // 8) % 4
            for other in (1, 0):
                shard = shard_of(to_x, to_y, (my_low + other) % 2, (core + line) % 2)

                @pl.when((shard != my_shard) | (tensor != my_tensor))
                def _():
                    pltpu.make_async_remote_copy(
                        src_ref=upd.at[tensor, shard],
                        dst_ref=out.at[y, my_low, x, core, my_tensor],
                        send_sem=back_send_sem,
                        recv_sem=back_recv_sem,
                        device_id=(shard, tensor),
                        device_id_type=MESH,
                    ).start()
            return carry

        lax.fori_loop(0, 32, to_line, 0)

    def step_and_send(step, carry):
        tensor = (my_tensor + 2 + step) % 4
        second_step(tensor)
        send_panel(tensor)
        return carry

    lax.fori_loop(0, 4, step_and_send, 0)
    stay = pltpu.make_async_copy(upd.at[my_tensor, my_shard], out.at[y, my_low, x, core, my_tensor], back_recv_sem)
    stay.start()

    sent = whole.at[pl.ds(0, 63)]
    rest = piece(whole, 0, 0)
    for sem in (send_sem, back_send_sem):
        pltpu.make_async_copy(sent, sent, sem).wait()
        for _ in range(3):
            pltpu.make_async_copy(rest, rest, sem).wait()
    pltpu.make_async_copy(out, out, back_recv_sem).wait()


def write_out(kept, out, kept_hbm, out_hbm, sem):
    copies = [pltpu.make_async_copy(kept, kept_hbm, sem.at[0]), pltpu.make_async_copy(out, out_hbm, sem.at[1])]
    for copy in copies:
        copy.start()
    for copy in copies:
        copy.wait()


def shards(grads, momentum):
    vmem = pl.BlockSpec(memory_space=pltpu.VMEM)
    hbm = pl.BlockSpec(memory_space=pltpu.HBM)
    piece = grads.shape[1:]
    by_column = OWNERS[:3] + (8,) + piece
    by_owner = OWNERS + piece
    block = (64, 16, 1024)
    square = (1024, 1024)
    kept, update = pl.pallas_call(
        kernel,
        name="muon",
        out_shape=(pltpu.VMEM(by_column, jnp.float32), pltpu.VMEM(by_owner, jnp.bfloat16)),
        in_specs=[hbm, hbm],
        out_specs=(vmem, vmem),
        scratch_shapes=[
            pltpu.VMEM(by_column, jnp.bfloat16),
            pltpu.VMEM(by_owner, jnp.bfloat16),
            pltpu.VMEM(block, jnp.bfloat16),
            pltpu.VMEM(square, jnp.bfloat16),
            pltpu.VMEM(square, jnp.bfloat16),
            pltpu.VMEM(block, jnp.bfloat16),
            pltpu.VMEM((4, 64, 16, 256), jnp.bfloat16),
            pltpu.SemaphoreType.DMA((2, 4)),
            pltpu.SemaphoreType.REGULAR,
            pltpu.SemaphoreType.DMA,
            pltpu.SemaphoreType.DMA,
            pltpu.SemaphoreType.DMA,
            pltpu.SemaphoreType.DMA,
        ],
        compiler_params=pltpu.CompilerParams(collective_id=0, has_side_effects=True, vmem_limit_bytes=57 * 2**20),
    )(grads.reshape(by_column), momentum.reshape(by_column))
    return pl.pallas_call(
        write_out,
        name="write_out",
        out_shape=(
            jax.ShapeDtypeStruct(momentum.shape, jnp.float32),
            jax.ShapeDtypeStruct(grads.shape, jnp.bfloat16),
        ),
        in_specs=[vmem, vmem],
        out_specs=(hbm, hbm),
        scratch_shapes=[pltpu.SemaphoreType.DMA((2,))],
        compiler_params=pltpu.CompilerParams(vmem_limit_bytes=2**20),
    )(kept.reshape(momentum.shape), update.reshape(grads.shape))


def solution(mesh):
    spec = P(None, "shard", "tensor")
    return jax.shard_map(shards, mesh=mesh, in_specs=(spec, spec), out_specs=(spec, spec), check_vma=False)
```

```python
import jax
import jax.numpy as jnp
from jax import lax
from jax.experimental import pallas as pl
from jax.experimental.pallas import tpu as pltpu
from jax.sharding import PartitionSpec as P

MESH = pl.DeviceIdType.MESH
NN = (((1,), (0,)), ((), ()))
NT = (((1,), (1,)), ((), ()))
A, B, C = 3.4445, -4.775, 2.0315
EARLY = 5
HOPS = (4, 1, -1, 2, -2, 3, -3, 0)
OWNERS = (4, 2, 4, 2, 4)


def dot(left, right, dims=NN):
    return lax.dot_general(left, right, dims, preferred_element_type=jnp.float32)


def kernel(grads, momentum, kept, out, fresh, nest, whole, gram, poly, mid, upd, load_sem, ready_sem, send_sem, recv_sem, back_send_sem, back_recv_sem):
    my_shard, my_tensor = lax.axis_index("shard"), lax.axis_index("tensor")
    x, y, core = (my_shard // 2) % 4, my_shard // 16, my_shard % 2
    my_low = (my_shard // 8) % 2
    z = my_tensor * 2 + my_low

    def depth(hop):
        to_z = (z + hop) % 8
        return to_z % 2, to_z // 2

    def shard_of(to_x, to_y, low, to_core):
        return to_y * 16 + low * 8 + to_x * 2 + to_core

    def column(step):
        return (x + step % 4) % 4, (y + step // 4) % 4

    def load(plane):
        to_y = (y + plane) % 4
        return (
            pltpu.make_async_copy(grads.at[to_y], fresh.at[to_y], load_sem.at[0, plane]),
            pltpu.make_async_copy(momentum.at[to_y], kept.at[to_y], load_sem.at[1, plane]),
        )

    for plane in range(4):
        for copy in load(plane):
            copy.start()

    barrier = pltpu.get_barrier_semaphore()
    for hop in (4, 3, -3, 2, -2, 1, -1):
        low, tensor = depth(hop)
        for to_core in (0, 1):
            pl.semaphore_signal(barrier, inc=1, device_id=(shard_of(x, y, low, to_core), tensor), device_id_type=MESH)

    def greet(step, carry):
        to_x, to_y = (x + 2 + step % 4) % 4, (y + 2 + step // 4) % 4

        @pl.when(step != 10)
        def _():
            for to_core in (0, 1):
                pl.semaphore_signal(barrier, inc=1, device_id=(shard_of(to_x, to_y, my_low, to_core), my_tensor), device_id_type=MESH)

        return carry

    lax.fori_loop(0, 16, greet, 0)
    pl.semaphore_signal(barrier, inc=1, device_id=(shard_of(x, y, my_low, 1 - core), my_tensor), device_id_type=MESH)

    def blend(step, carry):
        @pl.when(step % 4 == 0)
        def _():
            for copy in load(step // 4):
                copy.wait()

        to_x, to_y = column(step)
        for low in (0, 1):
            grads_f = fresh[to_y, low, to_x].astype(jnp.float32)
            momentum_next = 0.95 * kept[to_y, low, to_x] + grads_f
            kept[to_y, low, to_x] = momentum_next
            nest[to_y, low, to_x] = (grads_f + 0.95 * momentum_next).astype(jnp.bfloat16).reshape(2, 4, 16, 256)
        return carry

    def piece(ref, shard, tensor):
        return ref.at[shard, :, pl.ds(pl.multiple_of(tensor * 256, 256), 256)]

    def forward(to_x, to_y, hop, to_core):
        low, tensor = depth(hop)
        shard = shard_of(to_x, to_y, low, to_core)
        pltpu.make_async_remote_copy(
            src_ref=nest.at[to_y, low, to_x, to_core, tensor],
            dst_ref=piece(whole, my_shard, my_tensor),
            send_sem=send_sem,
            recv_sem=recv_sem,
            device_id=(shard, tensor),
            device_id_type=MESH,
        ).start()

    lax.fori_loop(0, 4, blend, 0)
    pl.semaphore_wait(barrier, 45)
    for hop in (4, 3, -3, 2, -2, 1, -1):
        low, tensor = depth(hop)
        pl.semaphore_signal(ready_sem, inc=1, device_id=(shard_of(x, y, low, core), tensor), device_id_type=MESH)

    for to_core in (0, 1):
        for hop in HOPS:
            if hop != 0:
                forward(x, y, hop, to_core)
    forward(x, y, 0, 1 - core)
    own = pltpu.make_async_copy(nest.at[y, my_low, x, core, my_tensor], piece(whole, my_shard, my_tensor), recv_sem)
    own.start()
    lax.fori_loop(4, EARLY + 1, blend, 0)
    pl.semaphore_wait(ready_sem, 7)

    def to_column(to_core, blending):
        def body(step, carry):
            to_x, to_y = column(step)
            for hop in HOPS:
                forward(to_x, to_y, hop, to_core)
            if blending:
                blend(step + EARLY, carry)
            return carry

        return body

    lax.fori_loop(1, 16 - EARLY, to_column(0, True), 0)
    lax.fori_loop(16 - EARLY, 16, to_column(0, False), 0)
    lax.fori_loop(1, 16, to_column(1, False), 0)
    pltpu.make_async_copy(whole, whole, recv_sem).wait()

    def columns(j):
        return pl.ds(pl.multiple_of(j * 256, 256), 256)

    def strip(ref, i):
        return ref[pl.ds(i * 16, 16)].reshape(256, 1024)

    def panel(ref, j):
        return ref[:, :, columns(j)].reshape(1024, 256)

    def square(ref):
        return ref[...].reshape(1024, 1024)

    def add_squares(i, total):
        part = strip(whole, i).astype(jnp.float32)
        return total + jnp.sum((part * part).reshape(32, 8, 1024), axis=0)

    total = lax.fori_loop(0, 4, add_squares, jnp.zeros((8, 1024), jnp.float32))
    scale = 1.0 / (jnp.sqrt(jnp.sum(total, keepdims=True)) + 1e-7)

    def first_gram(j, carry):
        gram[:, columns(j)] = (dot(square(whole), strip(whole, j), NT) * (scale * scale)).astype(jnp.bfloat16)
        return carry

    def make_poly(j, carry):
        part = gram[:, columns(j)]
        poly[:, columns(j)] = (B * part.astype(jnp.float32) + C * dot(gram[...], part)).astype(jnp.bfloat16)
        return carry

    def first_step(j, carry):
        part = panel(whole, j)
        value = A * part.astype(jnp.float32) + dot(poly[...], part)
        mid[:, :, columns(j)] = (value * scale).astype(jnp.bfloat16).reshape(64, 16, 256)
        return carry

    def second_gram(j, carry):
        gram[:, columns(j)] = dot(square(mid), strip(mid, j), NT).astype(jnp.bfloat16)
        return carry

    for body in (first_gram, make_poly, first_step, second_gram, make_poly):
        lax.fori_loop(0, 4, body, 0)

    def second_step(tensor):
        part = panel(mid, tensor)
        value = A * part.astype(jnp.float32) + dot(poly[...], part)
        upd[tensor] = (0.2 * 32.0 * value).astype(jnp.bfloat16).reshape(64, 16, 256)

    def send_panel(tensor):
        def to_line(line, carry):
            to_x, to_y = (x + line // 2) % 4, (y + line // 8) % 4
            for other in (1, 0):
                shard = shard_of(to_x, to_y, (my_low + other) % 2, (core + line) % 2)

                @pl.when((shard != my_shard) | (tensor != my_tensor))
                def _():
                    pltpu.make_async_remote_copy(
                        src_ref=upd.at[tensor, shard],
                        dst_ref=out.at[y, my_low, x, core, my_tensor],
                        send_sem=back_send_sem,
                        recv_sem=back_recv_sem,
                        device_id=(shard, tensor),
                        device_id_type=MESH,
                    ).start()
            return carry

        lax.fori_loop(0, 32, to_line, 0)

    def step_and_send(step, carry):
        tensor = (my_tensor + 2 + step) % 4
        second_step(tensor)
        send_panel(tensor)
        return carry

    lax.fori_loop(0, 4, step_and_send, 0)
    stay = pltpu.make_async_copy(upd.at[my_tensor, my_shard], out.at[y, my_low, x, core, my_tensor], back_recv_sem)
    stay.start()

    sent = whole.at[pl.ds(0, 63)]
    rest = piece(whole, 0, 0)
    for sem in (send_sem, back_send_sem):
        pltpu.make_async_copy(sent, sent, sem).wait()
        for _ in range(3):
            pltpu.make_async_copy(rest, rest, sem).wait()
    pltpu.make_async_copy(out, out, back_recv_sem).wait()


def write_out(kept, out, kept_hbm, out_hbm, sem):
    copies = [pltpu.make_async_copy(kept, kept_hbm, sem.at[0]), pltpu.make_async_copy(out, out_hbm, sem.at[1])]
    for copy in copies:
        copy.start()
    for copy in copies:
        copy.wait()


def shards(grads, momentum):
    vmem = pl.BlockSpec(memory_space=pltpu.VMEM)
    hbm = pl.BlockSpec(memory_space=pltpu.HBM)
    piece = grads.shape[1:]
    by_column = OWNERS[:3] + (8,) + piece
    by_owner = OWNERS + piece
    block = (64, 16, 1024)
    square = (1024, 1024)
    kept, update = pl.pallas_call(
        kernel,
        name="muon",
        out_shape=(pltpu.VMEM(by_column, jnp.float32), pltpu.VMEM(by_owner, jnp.bfloat16)),
        in_specs=[hbm, hbm],
        out_specs=(vmem, vmem),
        scratch_shapes=[
            pltpu.VMEM(by_column, jnp.bfloat16),
            pltpu.VMEM(by_owner, jnp.bfloat16),
            pltpu.VMEM(block, jnp.bfloat16),
            pltpu.VMEM(square, jnp.bfloat16),
            pltpu.VMEM(square, jnp.bfloat16),
            pltpu.VMEM(block, jnp.bfloat16),
            pltpu.VMEM((4, 64, 16, 256), jnp.bfloat16),
            pltpu.SemaphoreType.DMA((2, 4)),
            pltpu.SemaphoreType.REGULAR,
            pltpu.SemaphoreType.DMA,
            pltpu.SemaphoreType.DMA,
            pltpu.SemaphoreType.DMA,
            pltpu.SemaphoreType.DMA,
        ],
        compiler_params=pltpu.CompilerParams(collective_id=0, has_side_effects=True, vmem_limit_bytes=57 * 2**20),
    )(grads.reshape(by_column), momentum.reshape(by_column))
    return pl.pallas_call(
        write_out,
        name="write_out",
        out_shape=(
            jax.ShapeDtypeStruct(momentum.shape, jnp.float32),
            jax.ShapeDtypeStruct(grads.shape, jnp.bfloat16),
        ),
        in_specs=[vmem, vmem],
        out_specs=(hbm, hbm),
        scratch_shapes=[pltpu.SemaphoreType.DMA((2,))],
        compiler_params=pltpu.CompilerParams(vmem_limit_bytes=2**20),
    )(kept.reshape(momentum.shape), update.reshape(grads.shape))


def solution(mesh):
    spec = P(None, "shard", "tensor")
    return jax.shard_map(shards, mesh=mesh, in_specs=(spec, spec), out_specs=(spec, spec), check_vma=False)
```
